768 devices in a mesh: sec: 8 (over y_lo, core), blk: 96 (over x, y_hi, z).
Axes of the slice: x: 4, y: 8 (y_hi: 2, y_lo: 4; y = y_hi * 4 + y_lo), z: 12, core: 2. Of those that a mesh axis runs over, the one named last changes fastest.
Arguments:
- fluid_temp: float32 [8, 512, 12288], P(None, 'sec', 'blk'), may hold values from -6 to 6
- stream_velocity: float32 [8, 512, 12288], P(None, 'sec', 'blk'), may hold values from 0.2 to 1
- pitch_velocity: float32 [8, 512, 12288], P(None, 'sec', 'blk'), may hold values from -0.5 to 0.5
- film_coeff: float32 [512, 12288], P('sec', 'blk'), may hold values from 0.1 to 0.3
- solid_temp: float32 [8, 32, 12288], P('sec', None, 'blk'), may hold values from -6 to 6
- conductivity: float32 [8, 32, 12288], P('sec', None, 'blk'), may hold values from 0.5 to 2
- face_owner: int32 [8, 96, 64, 1], P('sec', 'blk'), may hold values from 0 to 95; in each aligned block of 64 rows (0 to 63, 64 to 127, ..., all dimensions but the last counted through in order) at most 2 rows name the same one
Outputs:
- fluid_out: float32 [8, 512, 12288], P(None, 'sec', 'blk')
- solid_out: float32 [8, 32, 12288], P('sec', None, 'blk')
The draws below stay inside these ranges and needn't reach their ends.
Inputs may be any that keep to these rules, and one draw needn't show every extreme that they name: `face_owner`: the 64 wall blocks of one device name any one owner at most 2 times; some device names some owner exactly 2 times.
All inputs are finite; a program needn't handle non-finite values.
Results may differ from the reference program's by a relative error of at most 0.0001.
Values sent between devices are 32-bit elements; how exact they have to be, the bound alone decides.
A program may use at most 32 MiB of HBM per device.

```python
import math
import jax
import jax.numpy as jnp
import numpy as np
from jax import lax

FZ = 8
FP = 64
FS = 128
SD = 32
SUB = 4
CAP = 2
NP = 512
NSTR = 12288
N_SEC = 8
N_BLK = 96


def level_of(rng, dims, cuts, least, high):
    level, own = 1.0, jax.random.fold_in(rng, 6)
    for position, blocks in cuts:
        heights = jnp.exp(jax.random.uniform(jax.random.fold_in(own, position), (blocks,), jnp.float32, least / len(cuts), high / len(cuts)))
        level = level * jnp.repeat(heights, dims[position] // blocks).reshape([-1 if axis == position else 1 for axis in range(len(dims))])
    return level


def shared_out(own_key, own, number, rows, number_of, top, limit, slope):
    order = jax.random.permutation(own_key, number_of)
    packed, ordinary = load_shares(number_of, rows * top, limit, slope, True), load_shares(number_of, rows * top, limit, slope, False)
    places = jnp.arange(number_of)

    def named(tallies, offset_by):
        used = int((tallies > 0).sum())
        fixed = max(1, used // 4)
        shifted = fixed + (places - fixed + offset_by * (used - fixed)) % max(1, number_of - fixed)
        return jnp.zeros((number_of,), jnp.int32).at[order[jnp.where(places < fixed, places, shifted)]].set(jnp.asarray(tallies, jnp.int32))

    tallies = jnp.where(number % 4 == 0, named(packed, number // 4), named(ordinary, number - number // 4 - 1))
    mixed = jax.random.permutation(jax.random.fold_in(own, 3), number_of)
    source_of, sink = mixed[0:number_of // 2 * 2:2], mixed[1:number_of // 2 * 2:2]
    room = jnp.minimum(tallies[source_of] - 1, limit - tallies[sink]) // 2
    room = jnp.where((source_of == order[0]) | (sink == order[0]) | (tallies[sink] == 0), 0, jnp.maximum(room, 0))
    shifted = jax.random.randint(jax.random.fold_in(own, 4), (number_of // 2,), 0, 1 << 20) % (room + 1)
    tallies = tallies.at[source_of].add(-shifted).at[sink].add(shifted)
    labels = jnp.searchsorted(jnp.cumsum(tallies), jnp.arange(rows * top), side="right").astype(jnp.int32)
    grid = labels.reshape(top, rows).T
    grid = grid[jax.random.permutation(jax.random.fold_in(own, 1), rows)]
    offset_by = jax.random.randint(jax.random.fold_in(own, 2), (rows, 1), 0, top)
    return jnp.take_along_axis(grid, (jnp.arange(top)[None, :] + offset_by) % top, axis=1)


def load_shares(number_of, total, bound, slope, full):
    portions = [(1 << 20) // math.isqrt(rank ** slope) + 1 for rank in range(1, number_of + 1)]
    largest = bound if full else min(bound, max(-(-total // number_of), total * portions[0] // sum(portions)))
    least = 1 if total - largest >= number_of - 1 else 0
    given, spare = [largest] + [least] * (number_of - 1), total - largest - least * (number_of - 1)
    while spare > 0:
        movable = [i for i in range(1, number_of) if given[i] < largest] or [i for i in range(1, number_of) if given[i] < bound]
        whole, budget = sum([portions[i] for i in movable]), spare
        for i in movable:
            extra = min(bound - given[i], max(1, budget * portions[i] // whole), spare)
            given[i] = given[i] + extra
            spare = spare - extra
    return np.array(given)


def centred(key, shape, scale, most, shards=(), held_as=jnp.bfloat16):
    entries = jax.random.normal(key, shape, jnp.float32) * scale
    if len(shards) > 0:
        entries = level_of(key, shape, shards, -0.22, 0.18) * entries
    return jnp.clip(entries, min=-most, max=most).astype(held_as)


def setup_inputs(seed: int = 0) -> dict:
    streams_of = jax.random.split(jax.random.key(seed), 8)
    fluid_temp = centred(streams_of[0], (FZ, NP, NSTR), 1.0, 6.0, ((1, 8), (2, 96)), jnp.float32)
    stream_velocity = jnp.clip(0.2 + 0.8 * jax.random.uniform(streams_of[1], (FZ, NP, NSTR), jnp.float32) ** level_of(streams_of[1], (FZ, NP, NSTR), ((1, 8), (2, 96)), -0.2, 0.2), 0.2, 1.0)
    pitch_velocity = jnp.clip(jax.random.uniform(streams_of[2], (FZ, NP, NSTR), jnp.float32, -0.5, 0.5) * level_of(streams_of[2], (FZ, NP, NSTR), ((1, 8), (2, 96)), -0.4, 0.0), -0.5, 0.5)
    film_coeff = jnp.clip(jnp.exp(math.log(0.3) - 1.0986123 * jax.random.uniform(streams_of[3], (NP, NSTR), jnp.float32) ** level_of(streams_of[3], (NP, NSTR), ((0, 8), (1, 96)), -0.2, 0.2)), 0.1, 0.3)
    solid_temp = centred(streams_of[4], (N_SEC, SD, NSTR), 1.0, 6.0, ((0, 8), (2, 96)), jnp.float32)
    conductivity = jnp.clip(jnp.exp(math.log(2.0) - 1.3862944 * jax.random.uniform(streams_of[5], (N_SEC, SD, NSTR), jnp.float32) ** level_of(streams_of[5], (N_SEC, SD, NSTR), ((0, 8), (2, 96)), -0.2, 0.2)), 0.5, 2.0)
    face_owner_keys = jax.random.split(jax.random.fold_in(streams_of[6], 1), N_SEC * N_BLK * FP // FP)
    face_owner_turns = jax.random.permutation(jax.random.fold_in(streams_of[6], 3), N_SEC * N_BLK * FP // FP)
    face_owner = jax.vmap(lambda own, number: shared_out(jax.random.fold_in(streams_of[6], 2), own, number, FP, N_BLK, 1, CAP, 2))(face_owner_keys, face_owner_turns).reshape((N_SEC, N_BLK, FP, 1))
    return {"fluid_temp": fluid_temp, "stream_velocity": stream_velocity, "pitch_velocity": pitch_velocity, "film_coeff": film_coeff, "solid_temp": solid_temp, "conductivity": conductivity, "face_owner": face_owner}


ADVECT = 0.4
SPREAD = 0.04
WALL = 0.4
SOLID_STEP = 0.04
COOLING = 0.5
COOLANT = -1.0


def fluid_update(fluid, stream_velocity, pitch_velocity, wall_flux, pitch_extended, stream_extended):
    pitch_prev = pitch_extended[:, :-2]
    pitch_next = pitch_extended[:, 2:]
    stream_prev = stream_extended[:, :, :-2]
    stream_next = stream_extended[:, :, 2:]
    span_prev = jnp.concatenate([fluid[:1], fluid[:-1]], 0)
    span_next = jnp.concatenate([fluid[1:], fluid[-1:]], 0)
    spread = SPREAD * (pitch_prev + pitch_next + stream_prev + stream_next + span_prev + span_next - 6.0 * fluid)
    carried = (-ADVECT * stream_velocity * (fluid - stream_prev)
               - ADVECT * jnp.maximum(pitch_velocity, 0.0) * (fluid - pitch_prev)
               + ADVECT * jnp.maximum(-pitch_velocity, 0.0) * (pitch_next - fluid))
    updated = fluid + spread + carried
    return updated.at[0].add(-WALL * wall_flux)


def solid_update(solid, conduct, inflow, solid_extended, conduct_extended):
    stream_prev = solid_extended[..., :-2]
    stream_next = solid_extended[..., 2:]
    conduct_prev = conduct_extended[..., :-2]
    conduct_next = conduct_extended[..., 2:]
    depth_prev = jnp.concatenate([solid[:, :1], solid[:, :-1]], 1)
    depth_next = jnp.concatenate([solid[:, 1:], solid[:, -1:]], 1)
    kdepth_prev = jnp.concatenate([conduct[:, :1], conduct[:, :-1]], 1)
    kdepth_next = jnp.concatenate([conduct[:, 1:], conduct[:, -1:]], 1)
    flow = (0.5 * (conduct + conduct_prev) * (stream_prev - solid)
            + 0.5 * (conduct + conduct_next) * (stream_next - solid)
            + 0.5 * (conduct + kdepth_prev) * (depth_prev - solid)
            + 0.5 * (conduct + kdepth_next) * (depth_next - solid))
    updated = solid + SOLID_STEP * flow
    updated = updated.at[:, 0].add(SOLID_STEP * inflow)
    updated = updated.at[:, -1].add(SOLID_STEP * COOLING * (COOLANT - solid[:, -1]))
    return updated


def reference(fluid_temp, stream_velocity, pitch_velocity, film_coeff, solid_temp, conductivity, face_owner):
    owners = face_owner[..., 0]
    onehot = (owners[..., None] == jnp.arange(N_BLK, dtype=jnp.int32)).astype(jnp.float32)
    film = film_coeff.reshape(N_SEC, FP, N_BLK, FS).transpose(0, 2, 1, 3)
    fluid = fluid_temp
    solid = solid_temp
    for subiter in range(SUB):
        wall_rows = solid[:, 0, :].reshape(N_SEC, N_BLK, FS)
        wall_temp = jnp.einsum("sbpo,sof->sbpf", onehot, wall_rows, precision=lax.Precision.HIGHEST)
        layer = fluid[0].reshape(N_SEC, FP, N_BLK, FS).transpose(0, 2, 1, 3)
        flux = film * (layer - wall_temp)
        inflow = jnp.einsum("sbpo,sbpf->sof", onehot, flux, precision=lax.Precision.HIGHEST).reshape(N_SEC, NSTR)
        wall_flux = flux.transpose(0, 2, 1, 3).reshape(NP, NSTR)
        pitch_extended = jnp.concatenate([fluid[:, -1:], fluid, fluid[:, :1]], 1)
        stream_extended = jnp.pad(fluid, ((0, 0), (0, 0), (1, 1)))
        conduct = conductivity * (1.0 + 0.25 * jnp.tanh(solid))
        solid_extended = jnp.pad(solid, ((0, 0), (0, 0), (1, 1)))
        conduct_extended = jnp.pad(conduct, ((0, 0), (0, 0), (1, 1)))
        fluid = fluid_update(fluid, stream_velocity, pitch_velocity, wall_flux, pitch_extended, stream_extended)
        solid = solid_update(solid, conduct, inflow, solid_extended, conduct_extended)
    return (fluid, solid)
```

```python
import jax
import jax.numpy as jnp
from jax import lax
from jax.experimental import pallas as pl
from jax.experimental.pallas import tpu as pltpu
from jax.sharding import PartitionSpec as P

SUB = 4
F32 = jnp.float32
MESH = pl.DeviceIdType.MESH

ADVECT = 0.4
SPREAD = 0.04
WALL = 0.4
SOLID_STEP = 0.04
COOLING = 0.5
COOLANT = -1.0

FZ, FP, FS, SD = 8, 64, 128, 32
N_SEC, N_BLK = 8, 96
NX, NY, NZ = 4, 2, 12
TILES = FP // 8
PLANE = [(2, 1), (1, 1), (3, 1), (0, 1), (2, 0), (1, 0), (3, 0), (0, 0)]
HIGHEST = lax.Precision.HIGHEST


def slot_of(dx, dy, dz):
    return (dx * NY + dy) * NZ + dz


def roll(value, shift, axis):
    return pltpu.roll(value, shift, axis)


def kernel(
    fluid_in, stream_in, pitch_in, film_in, solid_in, cond_in, owner_ref,
    fluid_out, solid_out,
    field, vel, coef, film, solid, cond, pick, place, base0, packed,
    g_send, g_recv, table, pitch_send, pitch_recv, edge_send, edge_recv, rim_send, rim_recv,
    io_sem, g_ssem, g_rsem, t_ssem, t_rsem, h_ssem, h_rsem, r_ssem, r_rsem,
):
    sec = lax.axis_index("sec")
    blk = lax.axis_index("blk")
    x, y, z = blk // (NY * NZ), lax.rem(blk // NZ, NY), lax.rem(blk, NZ)
    sec_ids = [lax.rem(sec + N_SEC - 1, N_SEC), lax.rem(sec + 1, N_SEC)]
    blk_ids = [lax.rem(blk + N_BLK - 1, N_BLK), lax.rem(blk + 1, N_BLK)]
    plane = {
        (dx, dy): lax.rem(x + dx, NX) * (NY * NZ) + lax.rem(y + dy, NY) * NZ for dx, dy in PLANE
    }

    def each_peer(act):
        def step(t, carry):
            half = (t + 1) // 2
            dz = 6 + half * (1 - 2 * lax.rem(t, 2))
            far = lax.rem(z + dz, NZ)
            for dx, dy in PLANE:
                act(plane[dx, dy] + far, slot_of(dx, dy, dz), slot_of((NX - dx) % NX, dy, NZ - dz))
            return carry

        lax.fori_loop(0, NZ - 1, step, 0)
        for dx, dy in PLANE[:-1]:
            act(plane[dx, dy] + z, slot_of(dx, dy, 0), slot_of((NX - dx) % NX, dy, 0))

    loads = [
        pltpu.make_async_copy(fluid_in, field.at[0, :, pl.ds(8, FP), :], io_sem.at[0]),
        pltpu.make_async_copy(film_in, film, io_sem.at[1]),
        pltpu.make_async_copy(solid_in.at[0], solid, io_sem.at[2]),
        pltpu.make_async_copy(cond_in.at[0], cond, io_sem.at[3]),
        pltpu.make_async_copy(stream_in, vel.at[0], io_sem.at[4]),
        pltpu.make_async_copy(pitch_in, vel.at[1], io_sem.at[5]),
    ]
    for copy in loads:
        copy.start()

    barrier = pltpu.get_barrier_semaphore()
    each_peer(
        lambda peer, there, here: pl.semaphore_signal(
            barrier, inc=1, device_id={"blk": peer}, device_id_type=MESH
        )
    )
    for target in sec_ids:
        pl.semaphore_signal(barrier, inc=1, device_id={"sec": target}, device_id_type=MESH)

    owner = owner_ref[0, 0]
    slot = slot_of(
        lax.rem(owner // (NY * NZ) - x + NX, NX),
        lax.rem(lax.rem(owner // NZ, NY) - y + NY, NY),
        lax.rem(lax.rem(owner, NZ) - z + NZ, NZ),
    )
    wide = jnp.broadcast_to(slot, (FP, 128))
    chosen = (wide == lax.broadcasted_iota(jnp.int32, (FP, 128), 1)).astype(F32)
    pick[...] = chosen[:, :N_BLK]
    place[...] = chosen.T[:N_BLK]

    lane = lax.broadcasted_iota(jnp.int32, (8, 128), 1)
    pair = lane // 2
    even = lax.rem(lane, 2) == 0
    wide_lane = lax.broadcasted_iota(jnp.int32, (FP, 128), 1)
    keep_low = (blk != 0).astype(F32)
    keep_high = (blk != N_BLK - 1).astype(F32)

    def gathered(k):
        return jnp.dot(
            pick[...], table.at[k].reshape(N_BLK, FS)[...], precision=HIGHEST,
            preferred_element_type=F32,
        )

    def placed(value):
        return jnp.dot(place[...], value, precision=HIGHEST, preferred_element_type=F32)

    def both_ends(tile, index):
        return jnp.where(pair == index, roll(tile, lax.rem(2 * index + 1, 128), 1), 0.0)

    def layer_ends(layer, q):
        total = both_ends(layer[0:8], q * TILES)
        for t in range(1, TILES):
            total = total + both_ends(layer[8 * t : 8 * t + 8], q * TILES + t)
        return total

    def joined(below, above):
        return jnp.where(even, roll(above, 127, 1) * keep_high, roll(below, 1, 1) * keep_low)

    def shifted(tile, ends, index):
        rim = roll(ends, lax.rem(255 - 2 * index, 128), 1)
        low = jnp.where(lane == 0, rim, roll(tile, 1, 1))
        high = jnp.where(lane == 127, rim, roll(tile, 127, 1))
        return low, high

    def send_halo(k):
        for i in range(2):
            pltpu.make_async_remote_copy(
                pitch_send.at[k, i], pitch_recv.at[k, 1 - i], h_ssem.at[k, i], h_rsem.at[k, 1 - i],
                device_id={"sec": sec_ids[i]}, device_id_type=MESH,
            ).start()
            pltpu.make_async_remote_copy(
                edge_send.at[k], edge_recv.at[k, 1 - i], h_ssem.at[k, 2 + i],
                h_rsem.at[k, 3 - i], device_id={"blk": blk_ids[i]}, device_id_type=MESH,
            ).start()

    def take_halo(k):
        for i in range(2):
            here = pitch_recv.at[k, i]
            pltpu.make_async_copy(here, here, h_rsem.at[k, i]).wait()
            here = edge_recv.at[k, i]
            pltpu.make_async_copy(here, here, h_rsem.at[k, 2 + i]).wait()
        for q in range(FZ):
            field[k % 2, q, 7:8, :] = pitch_recv[k, 0, q : q + 1, :]
            field[k % 2, q, FP + 8 : FP + 9, :] = pitch_recv[k, 1, q : q + 1, :]
        return joined(edge_recv[k, 0], edge_recv[k, 1])

    def send_rim(k):
        for i in range(2):
            pltpu.make_async_remote_copy(
                rim_send.at[k], rim_recv.at[k, 1 - i], r_ssem.at[k, i], r_rsem.at[k, 1 - i],
                device_id={"blk": blk_ids[i]}, device_id_type=MESH,
            ).start()

    def take_rim(k):
        for i in range(2):
            here = rim_recv.at[k, i]
            pltpu.make_async_copy(here, here, r_rsem.at[k, i]).wait()
        return joined(rim_recv[k, 0], rim_recv[k, 1])

    def send_flux(first, count, sem):
        def act(peer, there, here):
            for c in range(first, first + count):
                pltpu.make_async_remote_copy(
                    g_send.at[c, there], g_recv.at[c, here], g_ssem.at[sem], g_rsem.at[sem],
                    device_id={"blk": peer}, device_id_type=MESH,
                ).start()

        each_peer(act)

    def take_flux(first, count, sem):
        here = g_recv.at[pl.ds(first, count), pl.ds(1, N_BLK - 1)]
        pltpu.make_async_copy(here, here, g_rsem.at[sem]).wait()
        out = []
        for c in range(first, first + count):
            g_recv[c, 0] = g_send[c, 0]
            out.append(
                jnp.sum(g_recv.at[c].reshape(N_BLK, FS)[...], axis=0, keepdims=True)
            )
        return out

    def send_wall(k):
        def act(peer, there, here):
            pltpu.make_async_remote_copy(
                table.at[k, 0], table.at[k, here], t_ssem.at[k], t_rsem.at[k],
                device_id={"blk": peer}, device_id_type=MESH,
            ).start()

        each_peer(act)

    def take_wall(k):
        here = table.at[k, pl.ds(1, N_BLK - 1)]
        pltpu.make_async_copy(here, here, t_rsem.at[k]).wait()

    def stencil(k, q, ends):
        cur = k % 2
        centre = field[cur, q, pl.ds(8, FP), :]
        before = field[cur, q, pl.ds(7, FP), :]
        after = field[cur, q, pl.ds(9, FP), :]
        below = field[cur, jnp.maximum(q - 1, 0), pl.ds(8, FP), :]
        above = field[cur, jnp.minimum(q + 1, FZ - 1), pl.ds(8, FP), :]
        lows, highs = [], []
        for t in range(TILES):
            low, high = shifted(centre[8 * t : 8 * t + 8], ends, q * TILES + t)
            lows.append(low)
            highs.append(high)
        low, high = jnp.concatenate(lows, 0), jnp.concatenate(highs, 0)
        return (
            coef[0, q] * centre
            + coef[1, q] * before
            + coef[2, q] * after
            + coef[3, q] * low
            + SPREAD * (high + below + above)
        )

    def store_layer(k, q, layer):
        field[k % 2, q, pl.ds(8, FP), :] = layer
        if k < SUB:
            pitch_send[k, 0, pl.ds(q, 1), :] = layer[0:1]
            pitch_send[k, 1, pl.ds(q, 1), :] = layer[FP - 1 : FP]

    def wall_layer(k, ends):
        layer = stencil(k, 0, ends) - WALL * film[...] * field[k % 2, 0, pl.ds(8, FP), :]
        base0[...] = layer
        return layer

    def other_layers(k, ends):
        def step(q, total):
            layer = stencil(k, q, ends)
            store_layer(k + 1, q, layer)
            if k + 1 < SUB:
                total = total + layer_ends(layer, q)
            return total

        packed[...] = lax.fori_loop(1, FZ, step, jnp.zeros((8, 128), F32))

    def finish_layer(k):
        take_wall(k)
        layer = base0[...] + WALL * film[...] * gathered(k)
        store_layer(k + 1, 0, layer)
        if k + 1 < SUB:
            edge_send[k + 1] = packed[...] + layer_ends(layer, 0)
            send_halo(k + 1)

    def conduct_of(metal):
        return cond[...] * (1.0 + 0.25 * jnp.tanh(metal))

    def pack_rim(k, metal, conduct):
        total = jnp.zeros((8, 128), F32)
        for t in range(SD // 8):
            total = total + both_ends(metal[8 * t : 8 * t + 8], t)
            total = total + both_ends(conduct[8 * t : 8 * t + 8], SD // 8 + t)
        rim_send[k] = total

    row = lax.broadcasted_iota(jnp.int32, (SD, FS), 0)

    def metal_step(metal, conduct, ends):
        def neighbours(value, offset):
            lows, highs = [], []
            for t in range(SD // 8):
                low, high = shifted(value[8 * t : 8 * t + 8], ends, offset + t)
                lows.append(low)
                highs.append(high)
            up = jnp.where(row == 0, value, roll(value, 1, 0))
            down = jnp.where(row == SD - 1, value, roll(value, SD - 1, 0))
            return jnp.concatenate(lows, 0), jnp.concatenate(highs, 0), up, down

        flow = jnp.zeros((SD, FS), F32)
        for near, k_near in zip(neighbours(metal, 0), neighbours(conduct, SD // 8)):
            flow = flow + 0.5 * (conduct + k_near) * (near - metal)
        cooling = jnp.where(row == SD - 1, COOLING * (COOLANT - metal), 0.0)
        return metal + SOLID_STEP * (flow + cooling)

    def heated(metal, inflow):
        return metal + jnp.where(row == 0, SOLID_STEP * inflow, 0.0)

    def publish(k, metal):
        table[k, 0] = metal[0:1]
        conduct = conduct_of(metal)
        pack_rim(k, metal, conduct)
        return conduct

    for copy in loads[:4]:
        copy.wait()
    h = film[...]
    v = h * field[0, 0, pl.ds(8, FP), :]
    firsts = placed(jnp.concatenate([v, h, WALL * h * h], 1))
    for c, dest in enumerate((0, 1, 3)):
        g_send.at[dest].reshape(N_BLK, FS)[...] = firsts[:, FS * c : FS * c + FS]
    metal = solid[...]
    conduct = publish(0, metal)

    def first_ends(q, total):
        layer = field[0, q, pl.ds(8, FP), :]
        pitch_send[0, 0, pl.ds(q, 1), :] = layer[0:1]
        pitch_send[0, 1, pl.ds(q, 1), :] = layer[FP - 1 : FP]
        return total + layer_ends(layer, q)

    edge_send[0] = lax.fori_loop(0, FZ, first_ends, jnp.zeros((8, 128), F32))
    for copy in loads[4:]:
        copy.wait()

    def coefficients(q, carry):
        u, w = vel[0, q], vel[1, q]
        coef[0, q] = (1.0 - 6.0 * SPREAD) - ADVECT * (u + jnp.abs(w))
        coef[1, q] = SPREAD + ADVECT * jnp.maximum(w, 0.0)
        coef[2, q] = SPREAD + ADVECT * jnp.maximum(-w, 0.0)
        coef[3, q] = SPREAD + ADVECT * u
        return carry

    lax.fori_loop(0, FZ, coefficients, 0)
    pl.semaphore_wait(barrier, N_BLK - 1 + 2)

    def flux_ahead(dest, layer):
        g_send.at[dest].reshape(N_BLK, FS)[...] = placed(film[...] * layer)

    send_halo(0)
    send_wall(0)
    send_flux(0, 2, 0)
    send_rim(0)
    ends = take_halo(0)
    flux_ahead(2, wall_layer(0, ends))
    send_flux(2, 2, 1)
    other_layers(0, ends)
    calm = metal_step(metal, conduct, take_rim(0))
    finish_layer(0)
    g0, total_h = take_flux(0, 2, 0)
    wall0 = metal[0:1]
    metal = heated(calm, g0 - wall0 * total_h)
    conduct = publish(1, metal)
    send_wall(1)
    send_rim(1)
    ends = take_halo(1)
    flux_ahead(4, wall_layer(1, ends))
    send_flux(4, 1, 2)
    other_layers(1, ends)
    calm = metal_step(metal, conduct, take_rim(1))
    wall1 = metal[0:1]
    g1, total_f = take_flux(2, 2, 1)
    metal = heated(calm, g1 + wall0 * total_f - wall1 * total_h)
    conduct = publish(2, metal)
    send_wall(2)
    send_rim(2)
    finish_layer(1)
    calm = metal_step(metal, conduct, take_rim(2))
    wall2 = metal[0:1]
    ends = take_halo(2)
    flux_ahead(5, wall_layer(2, ends))
    send_flux(5, 1, 3)
    (g2,) = take_flux(4, 1, 2)
    metal = heated(calm, g2 + wall1 * total_f - wall2 * total_h)
    conduct = publish(3, metal)
    send_wall(3)
    send_rim(3)
    other_layers(2, ends)
    finish_layer(2)
    wall3 = metal[0:1]
    ends = take_halo(3)
    wall_layer(3, ends)
    other_layers(3, ends)
    rest = pltpu.make_async_copy(
        field.at[0, pl.ds(1, FZ - 1), pl.ds(8, FP), :], fluid_out.at[pl.ds(1, FZ - 1)], io_sem.at[0]
    )
    rest.start()
    calm = metal_step(metal, conduct, take_rim(3))
    finish_layer(3)
    last = pltpu.make_async_copy(
        field.at[0, 0, pl.ds(8, FP), :], fluid_out.at[0], io_sem.at[1]
    )
    last.start()
    (g3,) = take_flux(5, 1, 3)
    solid[...] = heated(calm, g3 + wall2 * total_f - wall3 * total_h)
    metal_copy = pltpu.make_async_copy(solid, solid_out.at[0], io_sem.at[2])
    metal_copy.start()

    for first, count, sem in ((0, 2, 0), (2, 2, 1), (4, 1, 2), (5, 1, 3)):
        sent = g_send.at[pl.ds(first, count), pl.ds(1, N_BLK - 1)]
        pltpu.make_async_copy(sent, sent, g_ssem.at[sem]).wait()
    for k in range(SUB):
        sent = table.at[k, pl.ds(1, N_BLK - 1)]
        pltpu.make_async_copy(sent, sent, t_ssem.at[k]).wait()
        for i in range(2):
            sent = pitch_send.at[k, i]
            pltpu.make_async_copy(sent, sent, h_ssem.at[k, i]).wait()
            sent = edge_send.at[k]
            pltpu.make_async_copy(sent, sent, h_ssem.at[k, 2 + i]).wait()
            sent = rim_send.at[k]
            pltpu.make_async_copy(sent, sent, r_ssem.at[k, i]).wait()
    rest.wait()
    last.wait()
    metal_copy.wait()


def local(
    fluid_temp, stream_velocity, pitch_velocity, film_coeff, solid_temp, conductivity, face_owner
):
    dma = pltpu.SemaphoreType.DMA
    anywhere = pl.BlockSpec(memory_space=pl.ANY)
    return pl.pallas_call(
        kernel,
        out_shape=(
            jax.ShapeDtypeStruct((FZ, FP, FS), F32),
            jax.ShapeDtypeStruct((1, SD, FS), F32),
        ),
        in_specs=[anywhere] * 6 + [pl.BlockSpec(memory_space=pltpu.VMEM)],
        out_specs=(anywhere, anywhere),
        scratch_shapes=[
            pltpu.VMEM((2, FZ, FP + 16, FS), F32),
            pltpu.VMEM((2, FZ, FP, FS), F32),
            pltpu.VMEM((4, FZ, FP, FS), F32),
            pltpu.VMEM((FP, FS), F32),
            pltpu.VMEM((SD, FS), F32),
            pltpu.VMEM((SD, FS), F32),
            pltpu.VMEM((FP, N_BLK), F32),
            pltpu.VMEM((N_BLK, FP), F32),
            pltpu.VMEM((FP, FS), F32),
            pltpu.VMEM((8, FS), F32),
            pltpu.VMEM((6, N_BLK, 1, FS), F32),
            pltpu.VMEM((6, N_BLK, 1, FS), F32),
            pltpu.VMEM((SUB, N_BLK, 1, FS), F32),
            pltpu.VMEM((SUB, 2, FZ, FS), F32),
            pltpu.VMEM((SUB, 2, FZ, FS), F32),
            pltpu.VMEM((SUB, 8, FS), F32),
            pltpu.VMEM((SUB, 2, 8, FS), F32),
            pltpu.VMEM((SUB, 8, FS), F32),
            pltpu.VMEM((SUB, 2, 8, FS), F32),
            dma((6,)), dma((4,)), dma((4,)), dma((SUB,)), dma((SUB,)),
            dma((SUB, 4)), dma((SUB, 4)), dma((SUB, 2)), dma((SUB, 2)),
        ],
        compiler_params=pltpu.CompilerParams(collective_id=0, has_side_effects=True),
    )(fluid_temp, stream_velocity, pitch_velocity, film_coeff, solid_temp, conductivity, face_owner)


def solution(mesh):
    placed = (
        P(None, "sec", "blk"),
        P(None, "sec", "blk"),
        P(None, "sec", "blk"),
        P("sec", "blk"),
        P("sec", None, "blk"),
        P("sec", None, "blk"),
        P("sec", "blk", None, None),
    )
    return jax.shard_map(
        local,
        mesh=mesh,
        in_specs=placed,
        out_specs=(P(None, "sec", "blk"), P("sec", None, "blk")),
        check_vma=False,
    )
```

```python
import jax
import jax.numpy as jnp
from jax import lax
from jax.experimental import pallas as pl
from jax.experimental.pallas import tpu as pltpu
from jax.sharding import PartitionSpec as P

SUB = 4
F32 = jnp.float32
BF16 = jnp.bfloat16
MESH = pl.DeviceIdType.MESH

ADVECT = 0.4
SPREAD = 0.04
WALL = 0.4
SOLID_STEP = 0.04
COOLING = 0.5
COOLANT = -1.0

FZ, FP, FS, SD = 8, 64, 128, 32
N_SEC, N_BLK = 8, 96
NX, NY, NZ = 4, 2, 12
TILES = FP // 8
PLANE = [(2, 1), (1, 1), (3, 1), (0, 1), (2, 0), (1, 0), (3, 0), (0, 0)]


def slot_of(dx, dy, dz):
    return (dx * NY + dy) * NZ + dz


def roll(value, shift, axis):
    return pltpu.roll(value, shift, axis)


def kernel(
    fluid_in, stream_in, pitch_in, film_in, solid_in, cond_in, owner_in,
    fluid_out, solid_out,
    field, vel, coef, film, solid, cond, owners, pick, place, base0,
    const_send, const_recv, edge_film, edge_fix,
    g_send, g_recv, table, pitch_send, pitch_recv, edge_send, edge_recv, rim_send, rim_recv,
    io_sem, g_ssem, g_rsem, t_ssem, t_rsem, h_ssem, h_rsem, r_ssem, r_rsem, c_ssem, c_rsem,
):
    sec = lax.axis_index("sec")
    blk = lax.axis_index("blk")
    x, y, z = blk // (NY * NZ), lax.rem(blk // NZ, NY), lax.rem(blk, NZ)
    sec_ids = [lax.rem(sec + N_SEC - 1, N_SEC), lax.rem(sec + 1, N_SEC)]
    blk_ids = [lax.rem(blk + N_BLK - 1, N_BLK), lax.rem(blk + 1, N_BLK)]
    plane = {
        (dx, dy): lax.rem(x + dx, NX) * (NY * NZ) + lax.rem(y + dy, NY) * NZ for dx, dy in PLANE
    }

    def each_peer(act):
        def step(t, carry):
            half = (t + 1) // 2
            dz = 6 + half * (1 - 2 * lax.rem(t, 2))
            far = lax.rem(z + dz, NZ)
            for dx, dy in PLANE:
                act(plane[dx, dy] + far, slot_of(dx, dy, dz), slot_of((NX - dx) % NX, dy, NZ - dz))
            return carry

        lax.fori_loop(0, NZ - 1, step, 0)
        for dx, dy in PLANE[:-1]:
            act(plane[dx, dy] + z, slot_of(dx, dy, 0), slot_of((NX - dx) % NX, dy, 0))

    loads = [
        pltpu.make_async_copy(owner_in, owners, io_sem.at[6]),
        pltpu.make_async_copy(fluid_in, field.at[0, :, pl.ds(8, FP), :], io_sem.at[0]),
        pltpu.make_async_copy(film_in, film, io_sem.at[1]),
        pltpu.make_async_copy(solid_in.at[0], solid, io_sem.at[2]),
        pltpu.make_async_copy(cond_in.at[0], cond, io_sem.at[3]),
        pltpu.make_async_copy(stream_in, vel.at[0], io_sem.at[4]),
        pltpu.make_async_copy(pitch_in, vel.at[1], io_sem.at[5]),
    ]
    for copy in loads:
        copy.start()

    barrier = pltpu.get_barrier_semaphore()
    each_peer(
        lambda peer, there, here: pl.semaphore_signal(
            barrier, inc=1, device_id={"blk": peer}, device_id_type=MESH
        )
    )
    for target in sec_ids:
        pl.semaphore_signal(barrier, inc=1, device_id={"sec": target}, device_id_type=MESH)

    loads[0].wait()
    owner = owners[...]

    def one_hot(owner):
        slot = slot_of(
            lax.rem(owner // (NY * NZ) - x + NX, NX),
            lax.rem(lax.rem(owner // NZ, NY) - y + NY, NY),
            lax.rem(lax.rem(owner, NZ) - z + NZ, NZ),
        )
        wide = jnp.broadcast_to(slot, (128, FP))
        return (wide == lax.broadcasted_iota(jnp.int32, (128, FP), 0)).astype(F32)

    chosen = one_hot(owner)
    place[...] = chosen[:N_BLK].astype(BF16)
    pick[0:FP] = chosen.T[:, :N_BLK].astype(BF16)

    lane = lax.broadcasted_iota(jnp.int32, (8, 128), 1)
    pair = lane // 2
    even = lax.rem(lane, 2) == 0
    wide_lane = lax.broadcasted_iota(jnp.int32, (FP, 128), 1)
    keep_low = (blk != 0).astype(F32)
    keep_high = (blk != N_BLK - 1).astype(F32)

    def selected(ones, value):
        high = value.astype(BF16)
        rest = value - high.astype(F32)
        middle = rest.astype(BF16)
        low = (rest - middle.astype(F32)).astype(BF16)
        dot = lambda part: jnp.dot(ones, part, preferred_element_type=F32)
        return (dot(low) + dot(middle)) + dot(high)

    def gathered(k, rows):
        return selected(pick[0:rows], table.at[k].reshape(N_BLK, FS)[...])

    def placed(value):
        return selected(place[...], value)

    def both_ends(tile, index):
        return jnp.where(pair == index, roll(tile, lax.rem(2 * index + 1, 128), 1), 0.0)

    def layer_ends(layer, q):
        total = both_ends(layer[0:8], q * TILES)
        for t in range(1, TILES):
            total = total + both_ends(layer[8 * t : 8 * t + 8], q * TILES + t)
        return total

    def joined(below, above):
        return jnp.where(even, roll(above, 127, 1) * keep_high, roll(below, 1, 1) * keep_low)

    def shifted(tile, ends, index):
        rim = roll(ends, lax.rem(255 - 2 * index, 128), 1)
        low = jnp.where(lane == 0, rim, roll(tile, 1, 1))
        high = jnp.where(lane == 127, rim, roll(tile, 127, 1))
        return low, high

    def send_pitch(k):
        for i in range(2):
            pltpu.make_async_remote_copy(
                pitch_send.at[k, i], pitch_recv.at[k, 1 - i], h_ssem.at[k, i], h_rsem.at[k, 1 - i],
                device_id={"sec": sec_ids[i]}, device_id_type=MESH,
            ).start()

    def send_const():
        for i in range(2):
            pltpu.make_async_remote_copy(
                const_send, const_recv.at[1 - i], c_ssem.at[i], c_rsem.at[1 - i],
                device_id={"blk": blk_ids[i]}, device_id_type=MESH,
            ).start()

    def take_const():
        for i in range(2):
            here = const_recv.at[i]
            pltpu.make_async_copy(here, here, c_rsem.at[i]).wait()
            beside = one_hot(const_recv[i, 1, 0:1, 0:FP].astype(jnp.int32))
            pick[FP * (i + 1) : FP * (i + 2)] = beside.T[:, :N_BLK].astype(BF16)
        edge_film[...] = joined(const_recv[0, 0], const_recv[1, 0])

    def send_edge(k):
        for i in range(2):
            pltpu.make_async_remote_copy(
                edge_send.at[k], edge_recv.at[k, 1 - i], h_ssem.at[k, 2 + i],
                h_rsem.at[k, 3 - i], device_id={"blk": blk_ids[i]}, device_id_type=MESH,
            ).start()

    def take_halo(k):
        for i in range(2):
            here = pitch_recv.at[k, i]
            pltpu.make_async_copy(here, here, h_rsem.at[k, i]).wait()
            here = edge_recv.at[k, i]
            pltpu.make_async_copy(here, here, h_rsem.at[k, 2 + i]).wait()
        for q in range(FZ):
            field[k % 2, q, 7:8, :] = pitch_recv[k, 0, q : q + 1, :]
            field[k % 2, q, FP + 8 : FP + 9, :] = pitch_recv[k, 1, q : q + 1, :]
        ends = joined(edge_recv[k, 0], edge_recv[k, 1])
        return ends + edge_fix[...] if k else ends

    def send_rim(k):
        for i in range(2):
            pltpu.make_async_remote_copy(
                rim_send.at[k], rim_recv.at[k, 1 - i], r_ssem.at[k, i], r_rsem.at[k, 1 - i],
                device_id={"blk": blk_ids[i]}, device_id_type=MESH,
            ).start()

    def take_rim(k):
        for i in range(2):
            here = rim_recv.at[k, i]
            pltpu.make_async_copy(here, here, r_rsem.at[k, i]).wait()
        return joined(rim_recv[k, 0], rim_recv[k, 1])

    def send_flux(first, count, sem):
        def act(peer, there, here):
            for c in range(first, first + count):
                pltpu.make_async_remote_copy(
                    g_send.at[c, there], g_recv.at[c, here], g_ssem.at[sem], g_rsem.at[sem],
                    device_id={"blk": peer}, device_id_type=MESH,
                ).start()

        each_peer(act)

    def take_flux(first, count, sem):
        here = g_recv.at[pl.ds(first, count), pl.ds(1, N_BLK - 1)]
        pltpu.make_async_copy(here, here, g_rsem.at[sem]).wait()
        out = []
        for c in range(first, first + count):
            g_recv[c, 0] = g_send[c, 0]
            out.append(
                jnp.sum(g_recv.at[c].reshape(N_BLK, FS)[...], axis=0, keepdims=True)
            )
        return out

    def send_first():
        def act(peer, there, here):
            pltpu.make_async_remote_copy(
                table.at[0, 0], table.at[0, here], t_ssem.at[0], t_rsem.at[0],
                device_id={"blk": peer}, device_id_type=MESH,
            ).start()
            for c in range(2):
                pltpu.make_async_remote_copy(
                    g_send.at[c, there], g_recv.at[c, here], g_ssem.at[0], g_rsem.at[0],
                    device_id={"blk": peer}, device_id_type=MESH,
                ).start()

        each_peer(act)

    def send_wall(k):
        def act(peer, there, here):
            pltpu.make_async_remote_copy(
                table.at[k, 0], table.at[k, here], t_ssem.at[k], t_rsem.at[k],
                device_id={"blk": peer}, device_id_type=MESH,
            ).start()

        each_peer(act)

    def take_wall(k):
        here = table.at[k, pl.ds(1, N_BLK - 1)]
        pltpu.make_async_copy(here, here, t_rsem.at[k]).wait()

    def stencil(k, q, ends):
        cur = k % 2
        centre = field[cur, q, pl.ds(8, FP), :]
        before = field[cur, q, pl.ds(7, FP), :]
        after = field[cur, q, pl.ds(9, FP), :]
        below = field[cur, jnp.maximum(q - 1, 0), pl.ds(8, FP), :]
        above = field[cur, jnp.minimum(q + 1, FZ - 1), pl.ds(8, FP), :]
        lows, highs = [], []
        for t in range(TILES):
            low, high = shifted(centre[8 * t : 8 * t + 8], ends, q * TILES + t)
            lows.append(low)
            highs.append(high)
        low, high = jnp.concatenate(lows, 0), jnp.concatenate(highs, 0)
        return (
            coef[0, q] * centre
            + coef[1, q] * before
            + coef[2, q] * after
            + coef[3, q] * low
            + SPREAD * (high + below + above)
        )

    def store_layer(k, q, layer):
        if k == SUB:
            fluid_out[q] = layer
        else:
            field[k % 2, q, pl.ds(8, FP), :] = layer
            pitch_send[k, 0, pl.ds(q, 1), :] = layer[0:1]
            pitch_send[k, 1, pl.ds(q, 1), :] = layer[FP - 1 : FP]

    def wall_layer(k, ends):
        layer = stencil(k, 0, ends) - WALL * film[...] * field[k % 2, 0, pl.ds(8, FP), :]
        base0[...] = layer
        return layer

    def other_layers(k, ends):
        def step(q, total):
            layer = stencil(k, q, ends)
            store_layer(k + 1, q, layer)
            if k + 1 < SUB:
                total = total + layer_ends(layer, q)
            return total

        total = lax.fori_loop(1, FZ, step, jnp.zeros((8, 128), F32))
        if k + 1 < SUB:
            edge_send[k + 1] = total + layer_ends(base0[...], 0)
            send_edge(k + 1)

    def finish_layer(k):
        take_wall(k)
        walls = gathered(k, 3 * FP if k + 1 < SUB else FP)
        layer = base0[...] + WALL * film[...] * walls[0:FP]
        store_layer(k + 1, 0, layer)
        if k + 1 < SUB:
            send_pitch(k + 1)
            total = jnp.zeros((8, 128), F32)
            for t in range(TILES):
                low = walls[FP + 8 * t : FP + 8 * t + 8]
                high = walls[2 * FP + 8 * t : 2 * FP + 8 * t + 8]
                total = jnp.where(lane == 2 * t + 1, roll(low, 2 * t + 2, 1), total)
                total = jnp.where(lane == 2 * t, roll(high, 2 * t, 1) if t else high, total)
            edge_fix[...] = edge_film[...] * total

    def conduct_of(metal):
        return cond[...] * (1.0 + 0.25 * jnp.tanh(metal))

    def pack_rim(k, metal, conduct):
        total = jnp.zeros((8, 128), F32)
        for t in range(SD // 8):
            total = total + both_ends(metal[8 * t : 8 * t + 8], t)
            total = total + both_ends(conduct[8 * t : 8 * t + 8], SD // 8 + t)
        rim_send[k] = total

    row = lax.broadcasted_iota(jnp.int32, (SD, FS), 0)

    def metal_step(metal, conduct, ends):
        def neighbours(value, offset):
            lows, highs = [], []
            for t in range(SD // 8):
                low, high = shifted(value[8 * t : 8 * t + 8], ends, offset + t)
                lows.append(low)
                highs.append(high)
            up = jnp.where(row == 0, value, roll(value, 1, 0))
            down = jnp.where(row == SD - 1, value, roll(value, SD - 1, 0))
            return jnp.concatenate(lows, 0), jnp.concatenate(highs, 0), up, down

        flow = jnp.zeros((SD, FS), F32)
        for near, k_near in zip(neighbours(metal, 0), neighbours(conduct, SD // 8)):
            flow = flow + 0.5 * (conduct + k_near) * (near - metal)
        cooling = jnp.where(row == SD - 1, COOLING * (COOLANT - metal), 0.0)
        return metal + SOLID_STEP * (flow + cooling)

    def heated(metal, inflow):
        return metal + jnp.where(row == 0, SOLID_STEP * inflow, 0.0)

    def publish(k, metal):
        table[k, 0] = metal[0:1]
        if k:
            send_wall(k)
        conduct = conduct_of(metal)
        pack_rim(k, metal, conduct)
        return conduct

    for copy in loads[1:5]:
        copy.wait()
    h = film[...]
    v = h * field[0, 0, pl.ds(8, FP), :]
    firsts = placed(jnp.concatenate([v, h, WALL * h * h], 1))
    for c, dest in enumerate((0, 1, 3)):
        g_send.at[dest].reshape(N_BLK, FS)[...] = firsts[:, FS * c : FS * c + FS]
    metal = solid[...]
    conduct = publish(0, metal)

    def first_ends(q, total):
        layer = field[0, q, pl.ds(8, FP), :]
        pitch_send[0, 0, pl.ds(q, 1), :] = layer[0:1]
        pitch_send[0, 1, pl.ds(q, 1), :] = layer[FP - 1 : FP]
        return total + layer_ends(layer, q)

    edge_send[0] = lax.fori_loop(0, FZ, first_ends, jnp.zeros((8, 128), F32))
    const_send[0] = layer_ends(WALL * h, 0)
    const_send[1] = jnp.concatenate([jnp.broadcast_to(owner, (8, FP)).astype(F32)] * 2, 1)
    for copy in loads[5:]:
        copy.wait()

    def coefficients(q, carry):
        u, w = vel[0, q], vel[1, q]
        coef[0, q] = (1.0 - 6.0 * SPREAD) - ADVECT * (u + jnp.abs(w))
        coef[1, q] = SPREAD + ADVECT * jnp.maximum(w, 0.0)
        coef[2, q] = SPREAD + ADVECT * jnp.maximum(-w, 0.0)
        coef[3, q] = SPREAD + ADVECT * u
        return carry

    lax.fori_loop(0, FZ, coefficients, 0)
    pl.semaphore_wait(barrier, N_BLK - 1 + 2)

    def flux_ahead(dest, layer):
        g_send.at[dest].reshape(N_BLK, FS)[...] = placed(film[...] * layer)

    send_pitch(0)
    send_edge(0)
    send_const()
    send_rim(0)
    send_first()
    ends = take_halo(0)
    flux_ahead(2, wall_layer(0, ends))
    other_layers(0, ends)
    send_flux(2, 2, 1)
    take_const()
    calm = metal_step(metal, conduct, take_rim(0))
    finish_layer(0)
    g0, total_h = take_flux(0, 2, 0)
    wall0 = metal[0:1]
    metal = heated(calm, g0 - wall0 * total_h)
    conduct = publish(1, metal)
    send_rim(1)
    ends = take_halo(1)
    flux_ahead(4, wall_layer(1, ends))
    send_flux(4, 1, 2)
    other_layers(1, ends)
    calm = metal_step(metal, conduct, take_rim(1))
    wall1 = metal[0:1]
    g1, total_f = take_flux(2, 2, 1)
    metal = heated(calm, g1 + wall0 * total_f - wall1 * total_h)
    conduct = publish(2, metal)
    send_rim(2)
    finish_layer(1)
    calm = metal_step(metal, conduct, take_rim(2))
    wall2 = metal[0:1]
    ends = take_halo(2)
    flux_ahead(5, wall_layer(2, ends))
    send_flux(5, 1, 3)
    (g2,) = take_flux(4, 1, 2)
    metal = heated(calm, g2 + wall1 * total_f - wall2 * total_h)
    conduct = publish(3, metal)
    send_rim(3)
    other_layers(2, ends)
    finish_layer(2)
    wall3 = metal[0:1]
    ends = take_halo(3)
    wall_layer(3, ends)
    other_layers(3, ends)
    calm = metal_step(metal, conduct, take_rim(3))
    finish_layer(3)
    (g3,) = take_flux(5, 1, 3)
    solid_out[0] = heated(calm, g3 + wall2 * total_f - wall3 * total_h)

    for first, count, sem in ((0, 2, 0), (2, 2, 1), (4, 1, 2), (5, 1, 3)):
        sent = g_send.at[pl.ds(first, count), pl.ds(1, N_BLK - 1)]
        pltpu.make_async_copy(sent, sent, g_ssem.at[sem]).wait()
    for k in range(SUB):
        sent = table.at[k, pl.ds(1, N_BLK - 1)]
        pltpu.make_async_copy(sent, sent, t_ssem.at[k]).wait()
        for i in range(2):
            sent = pitch_send.at[k, i]
            pltpu.make_async_copy(sent, sent, h_ssem.at[k, i]).wait()
            sent = edge_send.at[k]
            pltpu.make_async_copy(sent, sent, h_ssem.at[k, 2 + i]).wait()
            sent = rim_send.at[k]
            pltpu.make_async_copy(sent, sent, r_ssem.at[k, i]).wait()
    for i in range(2):
        pltpu.make_async_copy(const_send, const_send, c_ssem.at[i]).wait()


def write_out(fluid, metal, fluid_out, metal_out, sem):
    copies = [
        pltpu.make_async_copy(fluid, fluid_out, sem.at[0]),
        pltpu.make_async_copy(metal, metal_out, sem.at[1]),
    ]
    for copy in copies:
        copy.start()
    for copy in copies:
        copy.wait()


def local(
    fluid_temp, stream_velocity, pitch_velocity, film_coeff, solid_temp, conductivity, face_owner
):
    dma = pltpu.SemaphoreType.DMA
    anywhere = pl.BlockSpec(memory_space=pltpu.HBM)
    fluid, metal = pl.pallas_call(
        kernel,
        out_shape=(
            jax.ShapeDtypeStruct((FZ, FP, FS), F32),
            jax.ShapeDtypeStruct((1, SD, FS), F32),
        ),
        in_specs=[anywhere] * 7,
        out_specs=[pl.BlockSpec(memory_space=pltpu.VMEM)] * 2,
        scratch_shapes=[
            pltpu.VMEM((2, FZ, FP + 16, FS), F32),
            pltpu.VMEM((2, FZ, FP, FS), F32),
            pltpu.VMEM((4, FZ, FP, FS), F32),
            pltpu.VMEM((FP, FS), F32),
            pltpu.VMEM((SD, FS), F32),
            pltpu.VMEM((SD, FS), F32),
            pltpu.VMEM((1, FP), jnp.int32),
            pltpu.VMEM((3 * FP, N_BLK), BF16),
            pltpu.VMEM((N_BLK, FP), BF16),
            pltpu.VMEM((FP, FS), F32),
            pltpu.VMEM((2, 8, FS), F32),
            pltpu.VMEM((2, 2, 8, FS), F32),
            pltpu.VMEM((8, FS), F32),
            pltpu.VMEM((8, FS), F32),
            pltpu.VMEM((6, N_BLK, 1, FS), F32),
            pltpu.VMEM((6, N_BLK, 1, FS), F32),
            pltpu.VMEM((SUB, N_BLK, 1, FS), F32),
            pltpu.VMEM((SUB, 2, FZ, FS), F32),
            pltpu.VMEM((SUB, 2, FZ, FS), F32),
            pltpu.VMEM((SUB, 8, FS), F32),
            pltpu.VMEM((SUB, 2, 8, FS), F32),
            pltpu.VMEM((SUB, 8, FS), F32),
            pltpu.VMEM((SUB, 2, 8, FS), F32),
            dma((7,)), dma((4,)), dma((4,)), dma((SUB,)), dma((SUB,)),
            dma((SUB, 4)), dma((SUB, 4)), dma((SUB, 2)), dma((SUB, 2)), dma((2,)), dma((2,)),
        ],
        compiler_params=pltpu.CompilerParams(
            collective_id=0, has_side_effects=True, vmem_limit_bytes=16 << 20
        ),
    )(
        *(
            pltpu.with_memory_space_constraint(array, pltpu.HBM)
            for array in (
                fluid_temp, stream_velocity, pitch_velocity, film_coeff, solid_temp, conductivity,
                face_owner.reshape(1, FP),
            )
        )
    )
    return pl.pallas_call(
        write_out,
        out_shape=(
            jax.ShapeDtypeStruct((FZ, FP, FS), F32),
            jax.ShapeDtypeStruct((1, SD, FS), F32),
        ),
        in_specs=[pl.BlockSpec(memory_space=pltpu.VMEM)] * 2,
        out_specs=[anywhere] * 2,
        scratch_shapes=[dma((2,))],
        compiler_params=pltpu.CompilerParams(vmem_limit_bytes=1 << 20),
    )(fluid, metal)


def solution(mesh):
    placed = (
        P(None, "sec", "blk"),
        P(None, "sec", "blk"),
        P(None, "sec", "blk"),
        P("sec", "blk"),
        P("sec", None, "blk"),
        P("sec", None, "blk"),
        P("sec", "blk", None, None),
    )
    return jax.shard_map(
        local,
        mesh=mesh,
        in_specs=placed,
        out_specs=(P(None, "sec", "blk"), P("sec", None, "blk")),
        check_vma=False,
    )
```

```python
import jax
import jax.numpy as jnp
from jax import lax
from jax.experimental import pallas as pl
from jax.experimental.pallas import tpu as pltpu
from jax.sharding import PartitionSpec as P

SUB = 4
F32 = jnp.float32
BF16 = jnp.bfloat16
MESH = pl.DeviceIdType.MESH

ADVECT = 0.4
SPREAD = 0.04
WALL = 0.4
SOLID_STEP = 0.04
COOLING = 0.5
COOLANT = -1.0

FZ, FP, FS, SD = 8, 64, 128, 32
N_SEC, N_BLK = 8, 96
NX, NY, NZ = 4, 2, 12
TILES = FP // 8
PLANE = [(2, 1), (1, 1), (3, 1), (0, 1), (2, 0), (1, 0), (3, 0), (0, 0)]


def slot_of(dx, dy, dz):
    return (dx * NY + dy) * NZ + dz


def roll(value, shift, axis):
    return pltpu.roll(value, shift, axis)


def kernel(
    fluid_in, stream_in, pitch_in, film_in, solid_in, cond_in, owner_in,
    fluid_out, solid_out,
    field, vel, coef, film, solid, cond, owners, pick, place, base0,
    const_send, const_recv, edge_film, edge_fix,
    g_send, g_recv, table, pitch_send, pitch_recv, edge_send, edge_recv, rim_send, rim_recv,
    io_sem, g_ssem, g_rsem, t_ssem, t_rsem, h_ssem, h_rsem, r_ssem, r_rsem, c_ssem, c_rsem,
):
    sec = lax.axis_index("sec")
    blk = lax.axis_index("blk")
    x, y, z = blk // (NY * NZ), lax.rem(blk // NZ, NY), lax.rem(blk, NZ)
    sec_ids = [lax.rem(sec + N_SEC - 1, N_SEC), lax.rem(sec + 1, N_SEC)]
    blk_ids = [lax.rem(blk + N_BLK - 1, N_BLK), lax.rem(blk + 1, N_BLK)]
    plane = {
        (dx, dy): lax.rem(x + dx, NX) * (NY * NZ) + lax.rem(y + dy, NY) * NZ for dx, dy in PLANE
    }

    def each_peer(act):
        def step(t, carry):
            half = (t + 1) // 2
            dz = 6 + half * (1 - 2 * lax.rem(t, 2))
            far = lax.rem(z + dz, NZ)
            for dx, dy in PLANE:
                act(plane[dx, dy] + far, slot_of(dx, dy, dz), slot_of((NX - dx) % NX, dy, NZ - dz))
            return carry

        lax.fori_loop(0, NZ - 1, step, 0)
        for dx, dy in PLANE[:-1]:
            act(plane[dx, dy] + z, slot_of(dx, dy, 0), slot_of((NX - dx) % NX, dy, 0))

    loads = [
        pltpu.make_async_copy(owner_in, owners, io_sem.at[6]),
        pltpu.make_async_copy(fluid_in, field.at[0, :, pl.ds(8, FP), :], io_sem.at[0]),
        pltpu.make_async_copy(film_in, film, io_sem.at[1]),
        pltpu.make_async_copy(solid_in.at[0], solid, io_sem.at[2]),
        pltpu.make_async_copy(cond_in.at[0], cond, io_sem.at[3]),
        pltpu.make_async_copy(stream_in, vel.at[0], io_sem.at[4]),
        pltpu.make_async_copy(pitch_in, vel.at[1], io_sem.at[5]),
    ]
    for copy in loads:
        copy.start()

    barrier = pltpu.get_barrier_semaphore()
    each_peer(
        lambda peer, there, here: pl.semaphore_signal(
            barrier, inc=1, device_id={"blk": peer}, device_id_type=MESH
        )
    )
    for target in sec_ids:
        pl.semaphore_signal(barrier, inc=1, device_id={"sec": target}, device_id_type=MESH)

    loads[0].wait()
    owner = owners[...]

    def one_hot(owner):
        slot = slot_of(
            lax.rem(owner // (NY * NZ) - x + NX, NX),
            lax.rem(lax.rem(owner // NZ, NY) - y + NY, NY),
            lax.rem(lax.rem(owner, NZ) - z + NZ, NZ),
        )
        wide = jnp.broadcast_to(slot, (128, FP))
        return (wide == lax.broadcasted_iota(jnp.int32, (128, FP), 0)).astype(F32)

    chosen = one_hot(owner)
    place[...] = chosen[:N_BLK].astype(BF16)
    pick[0:FP] = chosen.T[:, :N_BLK].astype(BF16)

    lane = lax.broadcasted_iota(jnp.int32, (8, 128), 1)
    pair = lane // 2
    even = lax.rem(lane, 2) == 0
    wide_lane = lax.broadcasted_iota(jnp.int32, (FP, 128), 1)
    keep_low = (blk != 0).astype(F32)
    keep_high = (blk != N_BLK - 1).astype(F32)

    def selected(ones, value):
        high = value.astype(BF16)
        rest = value - high.astype(F32)
        middle = rest.astype(BF16)
        low = (rest - middle.astype(F32)).astype(BF16)
        dot = lambda part: jnp.dot(ones, part, preferred_element_type=F32)
        return (dot(low) + dot(middle)) + dot(high)

    def gathered(k, rows):
        return selected(pick[0:rows], table.at[k].reshape(N_BLK, FS)[...])

    def placed(value):
        return selected(place[...], value)

    def both_ends(tile, index):
        return jnp.where(pair == index, roll(tile, lax.rem(2 * index + 1, 128), 1), 0.0)

    def layer_ends(layer, q):
        total = both_ends(layer[0:8], q * TILES)
        for t in range(1, TILES):
            total = total + both_ends(layer[8 * t : 8 * t + 8], q * TILES + t)
        return total

    def joined(below, above):
        return jnp.where(even, roll(above, 127, 1) * keep_high, roll(below, 1, 1) * keep_low)

    def shifted(tile, ends, index):
        rim = roll(ends, lax.rem(255 - 2 * index, 128), 1)
        low = jnp.where(lane == 0, rim, roll(tile, 1, 1))
        high = jnp.where(lane == 127, rim, roll(tile, 127, 1))
        return low, high

    def send_pitch(k):
        for i in range(2):
            pltpu.make_async_remote_copy(
                pitch_send.at[k, i], pitch_recv.at[k, 1 - i], h_ssem.at[k, i], h_rsem.at[k, 1 - i],
                device_id={"sec": sec_ids[i]}, device_id_type=MESH,
            ).start()

    def send_const():
        for i in range(2):
            pltpu.make_async_remote_copy(
                const_send, const_recv.at[1 - i], c_ssem.at[i], c_rsem.at[1 - i],
                device_id={"blk": blk_ids[i]}, device_id_type=MESH,
            ).start()

    def take_const():
        for i in range(2):
            here = const_recv.at[i]
            pltpu.make_async_copy(here, here, c_rsem.at[i]).wait()
            beside = one_hot(const_recv[i, 1, 0:1, 0:FP].astype(jnp.int32))
            pick[FP * (i + 1) : FP * (i + 2)] = beside.T[:, :N_BLK].astype(BF16)
        edge_film[...] = joined(const_recv[0, 0], const_recv[1, 0])

    def send_edge(k):
        for i in range(2):
            pltpu.make_async_remote_copy(
                edge_send.at[k], edge_recv.at[k, 1 - i], h_ssem.at[k, 2 + i],
                h_rsem.at[k, 3 - i], device_id={"blk": blk_ids[i]}, device_id_type=MESH,
            ).start()

    def take_halo(k):
        for i in range(2):
            here = pitch_recv.at[k, i]
            pltpu.make_async_copy(here, here, h_rsem.at[k, i]).wait()
            here = edge_recv.at[k, i]
            pltpu.make_async_copy(here, here, h_rsem.at[k, 2 + i]).wait()
        for q in range(FZ):
            field[k % 2, q, 7:8, :] = pitch_recv[k, 0, q : q + 1, :]
            field[k % 2, q, FP + 8 : FP + 9, :] = pitch_recv[k, 1, q : q + 1, :]
        ends = joined(edge_recv[k, 0], edge_recv[k, 1])
        return ends + edge_fix[...] if k else ends

    def send_rim(k):
        for i in range(2):
            pltpu.make_async_remote_copy(
                rim_send.at[k], rim_recv.at[k, 1 - i], r_ssem.at[k, i], r_rsem.at[k, 1 - i],
                device_id={"blk": blk_ids[i]}, device_id_type=MESH,
            ).start()

    def take_rim(k):
        for i in range(2):
            here = rim_recv.at[k, i]
            pltpu.make_async_copy(here, here, r_rsem.at[k, i]).wait()
        return joined(rim_recv[k, 0], rim_recv[k, 1])

    def send_flux(first, count, sem):
        def act(peer, there, here):
            for c in range(first, first + count):
                pltpu.make_async_remote_copy(
                    g_send.at[c, there], g_recv.at[c, here], g_ssem.at[sem], g_rsem.at[sem],
                    device_id={"blk": peer}, device_id_type=MESH,
                ).start()

        each_peer(act)

    def take_flux(first, count, sem):
        here = g_recv.at[pl.ds(first, count), pl.ds(1, N_BLK - 1)]
        pltpu.make_async_copy(here, here, g_rsem.at[sem]).wait()
        out = []
        for c in range(first, first + count):
            g_recv[c, 0] = g_send[c, 0]
            out.append(
                jnp.sum(g_recv.at[c].reshape(N_BLK, FS)[...], axis=0, keepdims=True)
            )
        return out

    def send_first():
        def act(peer, there, here):
            pltpu.make_async_remote_copy(
                table.at[0, 0], table.at[0, here], t_ssem.at[0], t_rsem.at[0],
                device_id={"blk": peer}, device_id_type=MESH,
            ).start()
            for c in range(2):
                pltpu.make_async_remote_copy(
                    g_send.at[c, there], g_recv.at[c, here], g_ssem.at[0], g_rsem.at[0],
                    device_id={"blk": peer}, device_id_type=MESH,
                ).start()

        each_peer(act)

    def send_wall(k):
        def act(peer, there, here):
            pltpu.make_async_remote_copy(
                table.at[k, 0], table.at[k, here], t_ssem.at[k], t_rsem.at[k],
                device_id={"blk": peer}, device_id_type=MESH,
            ).start()

        each_peer(act)

    def take_wall(k):
        here = table.at[k, pl.ds(1, N_BLK - 1)]
        pltpu.make_async_copy(here, here, t_rsem.at[k]).wait()

    def stencil(k, q, ends):
        cur = k % 2
        centre = field[cur, q, pl.ds(8, FP), :]
        before = field[cur, q, pl.ds(7, FP), :]
        after = field[cur, q, pl.ds(9, FP), :]
        below = field[cur, jnp.maximum(q - 1, 0), pl.ds(8, FP), :]
        above = field[cur, jnp.minimum(q + 1, FZ - 1), pl.ds(8, FP), :]
        lows, highs = [], []
        for t in range(TILES):
            low, high = shifted(centre[8 * t : 8 * t + 8], ends, q * TILES + t)
            lows.append(low)
            highs.append(high)
        low, high = jnp.concatenate(lows, 0), jnp.concatenate(highs, 0)
        return (
            coef[0, q] * centre
            + coef[1, q] * before
            + coef[2, q] * after
            + coef[3, q] * low
            + SPREAD * (high + below + above)
        )

    def store_layer(k, q, layer):
        if k == SUB:
            fluid_out[q] = layer
        else:
            field[k % 2, q, pl.ds(8, FP), :] = layer
            pitch_send[k, 0, pl.ds(q, 1), :] = layer[0:1]
            pitch_send[k, 1, pl.ds(q, 1), :] = layer[FP - 1 : FP]

    def wall_layer(k, ends):
        layer = stencil(k, 0, ends) - WALL * film[...] * field[k % 2, 0, pl.ds(8, FP), :]
        base0[...] = layer
        return layer

    def other_layers(k, ends):
        def step(q, total):
            layer = stencil(k, q, ends)
            store_layer(k + 1, q, layer)
            if k + 1 < SUB:
                total = total + layer_ends(layer, q)
            return total

        total = lax.fori_loop(1, FZ, step, jnp.zeros((8, 128), F32))
        if k + 1 < SUB:
            edge_send[k + 1] = total + layer_ends(base0[...], 0)
            send_edge(k + 1)

    def finish_layer(k):
        take_wall(k)
        walls = gathered(k, 3 * FP if k + 1 < SUB else FP)
        layer = base0[...] + WALL * film[...] * walls[0:FP]
        store_layer(k + 1, 0, layer)
        if k + 1 < SUB:
            send_pitch(k + 1)
            total = jnp.zeros((8, 128), F32)
            for t in range(TILES):
                low = walls[FP + 8 * t : FP + 8 * t + 8]
                high = walls[2 * FP + 8 * t : 2 * FP + 8 * t + 8]
                total = jnp.where(lane == 2 * t + 1, roll(low, 2 * t + 2, 1), total)
                total = jnp.where(lane == 2 * t, roll(high, 2 * t, 1) if t else high, total)
            edge_fix[...] = edge_film[...] * total

    def conduct_of(metal):
        return cond[...] * (1.0 + 0.25 * jnp.tanh(metal))

    def pack_rim(k, metal, conduct):
        total = jnp.zeros((8, 128), F32)
        for t in range(SD // 8):
            total = total + both_ends(metal[8 * t : 8 * t + 8], t)
            total = total + both_ends(conduct[8 * t : 8 * t + 8], SD // 8 + t)
        rim_send[k] = total

    row = lax.broadcasted_iota(jnp.int32, (SD, FS), 0)

    def metal_step(metal, conduct, ends):
        def neighbours(value, offset):
            lows, highs = [], []
            for t in range(SD // 8):
                low, high = shifted(value[8 * t : 8 * t + 8], ends, offset + t)
                lows.append(low)
                highs.append(high)
            up = jnp.where(row == 0, value, roll(value, 1, 0))
            down = jnp.where(row == SD - 1, value, roll(value, SD - 1, 0))
            return jnp.concatenate(lows, 0), jnp.concatenate(highs, 0), up, down

        flow = jnp.zeros((SD, FS), F32)
        for near, k_near in zip(neighbours(metal, 0), neighbours(conduct, SD // 8)):
            flow = flow + 0.5 * (conduct + k_near) * (near - metal)
        cooling = jnp.where(row == SD - 1, COOLING * (COOLANT - metal), 0.0)
        return metal + SOLID_STEP * (flow + cooling)

    def heated(metal, inflow):
        return metal + jnp.where(row == 0, SOLID_STEP * inflow, 0.0)

    def publish(k, metal):
        table[k, 0] = metal[0:1]
        if k % 2:
            send_wall(k)
        conduct = conduct_of(metal)
        pack_rim(k, metal, conduct)
        return conduct

    for copy in loads[1:5]:
        copy.wait()
    h = film[...]
    v = h * field[0, 0, pl.ds(8, FP), :]
    firsts = placed(jnp.concatenate([v, h, WALL * h * h], 1))
    for c, dest in enumerate((0, 1, 3)):
        g_send.at[dest].reshape(N_BLK, FS)[...] = firsts[:, FS * c : FS * c + FS]
    metal = solid[...]
    conduct = publish(0, metal)

    def first_ends(q, total):
        layer = field[0, q, pl.ds(8, FP), :]
        pitch_send[0, 0, pl.ds(q, 1), :] = layer[0:1]
        pitch_send[0, 1, pl.ds(q, 1), :] = layer[FP - 1 : FP]
        return total + layer_ends(layer, q)

    edge_send[0] = lax.fori_loop(0, FZ, first_ends, jnp.zeros((8, 128), F32))
    const_send[0] = layer_ends(WALL * h, 0)
    const_send[1] = jnp.concatenate([jnp.broadcast_to(owner, (8, FP)).astype(F32)] * 2, 1)
    for copy in loads[5:]:
        copy.wait()

    def coefficients(q, carry):
        u, w = vel[0, q], vel[1, q]
        coef[0, q] = (1.0 - 6.0 * SPREAD) - ADVECT * (u + jnp.abs(w))
        coef[1, q] = SPREAD + ADVECT * jnp.maximum(w, 0.0)
        coef[2, q] = SPREAD + ADVECT * jnp.maximum(-w, 0.0)
        coef[3, q] = SPREAD + ADVECT * u
        return carry

    lax.fori_loop(0, FZ, coefficients, 0)
    pl.semaphore_wait(barrier, N_BLK - 1 + 2)

    def flux_ahead(dest, layer):
        g_send.at[dest].reshape(N_BLK, FS)[...] = placed(film[...] * layer)

    send_pitch(0)
    send_edge(0)
    send_const()
    send_rim(0)
    send_first()
    ends = take_halo(0)
    flux_ahead(2, wall_layer(0, ends))
    other_layers(0, ends)
    send_flux(2, 2, 1)
    take_const()
    calm = metal_step(metal, conduct, take_rim(0))
    finish_layer(0)
    g0, total_h = take_flux(0, 2, 0)
    wall0 = metal[0:1]
    metal = heated(calm, g0 - wall0 * total_h)
    conduct = publish(1, metal)
    send_rim(1)
    ends = take_halo(1)
    flux_ahead(4, wall_layer(1, ends))
    send_flux(4, 1, 2)
    other_layers(1, ends)
    calm = metal_step(metal, conduct, take_rim(1))
    wall1 = metal[0:1]
    g1, total_f = take_flux(2, 2, 1)
    metal = heated(calm, g1 + wall0 * total_f - wall1 * total_h)
    conduct = publish(2, metal)
    send_rim(2)
    finish_layer(1)
    send_wall(2)
    calm = metal_step(metal, conduct, take_rim(2))
    wall2 = metal[0:1]
    (g2,) = take_flux(4, 1, 2)
    metal = heated(calm, g2 + wall1 * total_f - wall2 * total_h)
    conduct = publish(3, metal)
    send_rim(3)
    ends = take_halo(2)
    flux_ahead(5, wall_layer(2, ends))
    send_flux(5, 1, 3)
    other_layers(2, ends)
    finish_layer(2)
    wall3 = metal[0:1]
    ends = take_halo(3)
    wall_layer(3, ends)
    other_layers(3, ends)
    calm = metal_step(metal, conduct, take_rim(3))
    finish_layer(3)
    (g3,) = take_flux(5, 1, 3)
    solid_out[0] = heated(calm, g3 + wall2 * total_f - wall3 * total_h)

    for first, count, sem in ((0, 2, 0), (2, 2, 1), (4, 1, 2), (5, 1, 3)):
        sent = g_send.at[pl.ds(first, count), pl.ds(1, N_BLK - 1)]
        pltpu.make_async_copy(sent, sent, g_ssem.at[sem]).wait()
    for k in range(SUB):
        sent = table.at[k, pl.ds(1, N_BLK - 1)]
        pltpu.make_async_copy(sent, sent, t_ssem.at[k]).wait()
        for i in range(2):
            sent = pitch_send.at[k, i]
            pltpu.make_async_copy(sent, sent, h_ssem.at[k, i]).wait()
            sent = edge_send.at[k]
            pltpu.make_async_copy(sent, sent, h_ssem.at[k, 2 + i]).wait()
            sent = rim_send.at[k]
            pltpu.make_async_copy(sent, sent, r_ssem.at[k, i]).wait()
    for i in range(2):
        pltpu.make_async_copy(const_send, const_send, c_ssem.at[i]).wait()


def write_out(fluid, metal, fluid_out, metal_out, sem):
    copies = [
        pltpu.make_async_copy(fluid, fluid_out, sem.at[0]),
        pltpu.make_async_copy(metal, metal_out, sem.at[1]),
    ]
    for copy in copies:
        copy.start()
    for copy in copies:
        copy.wait()


def local(
    fluid_temp, stream_velocity, pitch_velocity, film_coeff, solid_temp, conductivity, face_owner
):
    dma = pltpu.SemaphoreType.DMA
    anywhere = pl.BlockSpec(memory_space=pltpu.HBM)
    fluid, metal = pl.pallas_call(
        kernel,
        out_shape=(
            jax.ShapeDtypeStruct((FZ, FP, FS), F32),
            jax.ShapeDtypeStruct((1, SD, FS), F32),
        ),
        in_specs=[anywhere] * 7,
        out_specs=[pl.BlockSpec(memory_space=pltpu.VMEM)] * 2,
        scratch_shapes=[
            pltpu.VMEM((2, FZ, FP + 16, FS), F32),
            pltpu.VMEM((2, FZ, FP, FS), F32),
            pltpu.VMEM((4, FZ, FP, FS), F32),
            pltpu.VMEM((FP, FS), F32),
            pltpu.VMEM((SD, FS), F32),
            pltpu.VMEM((SD, FS), F32),
            pltpu.VMEM((1, FP), jnp.int32),
            pltpu.VMEM((3 * FP, N_BLK), BF16),
            pltpu.VMEM((N_BLK, FP), BF16),
            pltpu.VMEM((FP, FS), F32),
            pltpu.VMEM((2, 8, FS), F32),
            pltpu.VMEM((2, 2, 8, FS), F32),
            pltpu.VMEM((8, FS), F32),
            pltpu.VMEM((8, FS), F32),
            pltpu.VMEM((6, N_BLK, 1, FS), F32),
            pltpu.VMEM((6, N_BLK, 1, FS), F32),
            pltpu.VMEM((SUB, N_BLK, 1, FS), F32),
            pltpu.VMEM((SUB, 2, FZ, FS), F32),
            pltpu.VMEM((SUB, 2, FZ, FS), F32),
            pltpu.VMEM((SUB, 8, FS), F32),
            pltpu.VMEM((SUB, 2, 8, FS), F32),
            pltpu.VMEM((SUB, 8, FS), F32),
            pltpu.VMEM((SUB, 2, 8, FS), F32),
            dma((7,)), dma((4,)), dma((4,)), dma((SUB,)), dma((SUB,)),
            dma((SUB, 4)), dma((SUB, 4)), dma((SUB, 2)), dma((SUB, 2)), dma((2,)), dma((2,)),
        ],
        compiler_params=pltpu.CompilerParams(
            collective_id=0, has_side_effects=True, vmem_limit_bytes=16 << 20
        ),
    )(
        *(
            pltpu.with_memory_space_constraint(array, pltpu.HBM)
            for array in (
                fluid_temp, stream_velocity, pitch_velocity, film_coeff, solid_temp, conductivity,
                face_owner.reshape(1, FP),
            )
        )
    )
    return pl.pallas_call(
        write_out,
        out_shape=(
            jax.ShapeDtypeStruct((FZ, FP, FS), F32),
            jax.ShapeDtypeStruct((1, SD, FS), F32),
        ),
        in_specs=[pl.BlockSpec(memory_space=pltpu.VMEM)] * 2,
        out_specs=[anywhere] * 2,
        scratch_shapes=[dma((2,))],
        compiler_params=pltpu.CompilerParams(vmem_limit_bytes=1 << 20),
    )(fluid, metal)


def solution(mesh):
    placed = (
        P(None, "sec", "blk"),
        P(None, "sec", "blk"),
        P(None, "sec", "blk"),
        P("sec", "blk"),
        P("sec", None, "blk"),
        P("sec", None, "blk"),
        P("sec", "blk", None, None),
    )
    return jax.shard_map(
        local,
        mesh=mesh,
        in_specs=placed,
        out_specs=(P(None, "sec", "blk"), P("sec", None, "blk")),
        check_vma=False,
    )
```
